512 devices in a mesh: section: 16 (over x, z_lo), dp: 32 (over z_hi, y, core).
Axes of the slice: x: 4, y: 4, z: 16 (z_hi: 4, z_lo: 4; z = z_hi * 4 + z_lo), core: 2. Of those that a mesh axis runs over, the one named last changes fastest.
Arguments:
- activations: bfloat16 [16, 4096, 8192], P('section', 'dp'), may hold values from -6 to 6
- out_grads: bfloat16 [16, 4096, 1024], P('section', 'dp'), may hold values from -1.5 to 1.5
- in_basis: bfloat16 [16, 8192, 256], P('section', 'dp'), may hold values from -0.375 to 0.375
- out_basis: bfloat16 [16, 1024, 1024], P('section', 'dp'), may hold values from -0.1875 to 0.1875
- curvature: bfloat16 [16, 1024, 8192], P('section', None, 'dp'), may hold values from 2 to 32
- left_factors: bfloat16 [16, 32, 32, 1024], P('section', 'dp'), may hold values from -0.1875 to 0.1875
- right_factors: bfloat16 [16, 32, 32, 8192], P('section', None, None, 'dp'), may hold values from -0.0625 to 0.0625
- sequence_ids: int32 [32], replicated, may hold values from 0 to 31, each once
- query_order: int32 [32], replicated, may hold values from 0 to 31, each once
Outputs:
- influence: float32 [16, 32, 32], P('section', 'dp')
The draws below stay inside these ranges and needn't reach their ends.
Inputs may be any that keep to these rules, and one draw needn't show every extreme that they name: `sequence_ids`: a permutation: each output row receives exactly one training sequence. `query_order`: a permutation: each query is stored in exactly one slot.
All inputs are finite; a program needn't handle non-finite values.
Results may differ from the reference program's by a relative error of at most 0.0057.
Values may be sent and summed in bfloat16 or wider, within the bound.
A program may use at most 128 MiB of HBM per device.

```python
import math
import jax
import jax.numpy as jnp
from jax import lax

D = 8192
DOUT = 1024
BLK = 256
RANK = 32
SEQ_LEN = 128
LAYERS = 16
SEQS = 32
TOKENS = 4096
QUERIES = 32


def shard_levels(key, extent, split, least, top_value):
    gain, own = 1.0, jax.random.fold_in(key, 6)
    for position, blocks in split:
        steps = jnp.exp(jax.random.uniform(jax.random.fold_in(own, position), (blocks,), jnp.float32, least / len(split), top_value / len(split)))
        gain = gain * jnp.repeat(steps, extent[position] // blocks).reshape([-1 if axis == position else 1 for axis in range(len(extent))])
    return gain


def gaussian(stream_key, dims, width, reach, cuts=(), held_as=jnp.bfloat16):
    factor_of = shard_levels(stream_key, dims, cuts, -0.22, 0.18) if cuts else 1.0
    values = jax.random.normal(stream_key, dims, jnp.float32) * width * factor_of
    return jnp.minimum(jnp.maximum(values, -reach), reach).astype(held_as)


def setup_inputs(seed: int = 0) -> dict:
    streams_of = jax.random.split(jax.random.key(seed), 10)
    activations = gaussian(streams_of[0], (LAYERS, TOKENS, D), 1.0, 6.0, ((0, 16), (1, 32)))
    out_grads = gaussian(streams_of[1], (LAYERS, TOKENS, DOUT), 0.25, 1.5, ((0, 16), (1, 32)))
    in_basis = gaussian(streams_of[2], (LAYERS, D, BLK), BLK ** -0.5, 0.375, ((0, 16), (1, 32)))
    out_basis = gaussian(streams_of[3], (LAYERS, DOUT, DOUT), DOUT ** -0.5, 0.1875, ((0, 16), (1, 32)))
    curvature = jnp.clip(jnp.exp(math.log(32.0) - 2.7725887 * jax.random.uniform(streams_of[4], (LAYERS, DOUT, D), jnp.float32) ** shard_levels(streams_of[4], (LAYERS, DOUT, D), ((0, 16), (2, 32)), -0.2, 0.2)), 2.0, 32.0).astype(jnp.bfloat16)
    left_factors = gaussian(streams_of[5], (LAYERS, QUERIES, RANK, DOUT), DOUT ** -0.5, 0.1875, ((0, 16), (1, 32)))
    right_factors = gaussian(streams_of[6], (LAYERS, QUERIES, RANK, D), D ** -0.5, 0.0625, ((0, 16), (3, 32)))
    sequence_ids = jax.random.permutation(streams_of[7], SEQS).astype(jnp.int32)
    query_order = jax.random.permutation(streams_of[8], QUERIES).astype(jnp.int32)
    return {"activations": activations, "out_grads": out_grads, "in_basis": in_basis, "out_basis": out_basis, "curvature": curvature, "left_factors": left_factors, "right_factors": right_factors, "sequence_ids": sequence_ids, "query_order": query_order}


def layer_scores(operands):
    activations, out_grads, in_basis, out_basis, curvature, left_factors, right_factors = operands
    n_blocks = D // BLK
    rotated_acts = jnp.einsum("tbi,bij->tbj", activations.reshape(TOKENS, n_blocks, BLK).astype(jnp.float32), in_basis.reshape(n_blocks, BLK, BLK).astype(jnp.float32))
    rotated_acts = rotated_acts.astype(jnp.bfloat16).reshape(SEQS, SEQ_LEN, D)
    rotated_grads = jnp.dot(out_grads.astype(jnp.float32), out_basis.astype(jnp.float32), preferred_element_type=jnp.float32)
    rotated_grads = rotated_grads.astype(jnp.bfloat16).reshape(SEQS, SEQ_LEN, DOUT)
    divisor = curvature.astype(jnp.float32)

    def one_query(factors):
        product = jnp.dot(factors[0].astype(jnp.float32).T, factors[1].astype(jnp.float32), preferred_element_type=jnp.float32)
        return product.astype(jnp.bfloat16).reshape(DOUT * D)

    query_mats = lax.map(one_query, (left_factors, right_factors))

    def one_sequence(pieces):
        gradient = jnp.dot(pieces[0].astype(jnp.float32).T, pieces[1].astype(jnp.float32), preferred_element_type=jnp.float32)
        return (gradient / divisor).astype(jnp.bfloat16).reshape(DOUT * D)

    scaled = lax.map(one_sequence, (rotated_grads, rotated_acts))
    return jnp.dot(scaled.astype(jnp.float32), query_mats.astype(jnp.float32).T, preferred_element_type=jnp.float32)


def reference(activations, out_grads, in_basis, out_basis, curvature, left_factors, right_factors, sequence_ids, query_order):
    scores = lax.map(layer_scores, (activations, out_grads, in_basis, out_basis, curvature, left_factors, right_factors))
    row_pick = (sequence_ids[None, :] == jnp.arange(SEQS, dtype=jnp.int32)[:, None]).astype(jnp.float32)
    col_pick = (query_order[:, None] == jnp.arange(QUERIES, dtype=jnp.int32)[None, :]).astype(jnp.float32)
    placed = jnp.einsum("mn,lnk,kq->lmq", row_pick, scores, col_pick, precision=lax.Precision.HIGHEST)
    return jnp.flip(jnp.cumsum(jnp.flip(placed, 0), axis=0), 0)
```

```python
import jax
import jax.numpy as jnp
from jax import lax
from jax.experimental import pallas as pl
from jax.experimental.pallas import tpu as pltpu
from jax.sharding import PartitionSpec as P

MESH = pl.DeviceIdType.MESH
F32 = jnp.float32
BF16 = jnp.bfloat16
HI = lax.Precision.HIGHEST


def kernel(
    acts,
    grads,
    in_basis,
    out_basis,
    curv,
    left,
    right,
    seq_ids,
    q_order,
    out,
    small,
    big,
    cols,
    basis_v,
    left_v,
    ub_v,
    curv_v,
    inv_v,
    right_v,
    scaled_v,
    part_v,
    rows_v,
    row_send,
    row_recv,
    sec_send,
    sec_recv,
    small_ss,
    small_rs,
    big_ss,
    big_rs,
    col_ss,
    col_rs,
    row_ss,
    row_rs,
    sec_ss,
    sec_rs,
    loc,
):
    n_dev = 32
    n_sec = 16
    me = lax.axis_index("dp")
    sec = lax.axis_index("section")
    z = me // 8
    sub = me % 8
    y = sub // 2
    c = sub % 2
    step = 1 - 2 * c
    width = cols.shape[2]

    def slot(dz, dy, core):
        return ((z + dz + 8) % 4) * 8 + ((y + dy + 8) % 4) * 2 + core

    partner = slot(0, 0, 1 - c)

    own_cols = pl.ds(pl.multiple_of(me * width, width), width)
    l_u = pltpu.make_async_copy(out_basis, small.at[me, pl.ds(0, 32)], loc.at[0])
    l_l = pltpu.make_async_copy(left, small.at[me, pl.ds(32, 32)], loc.at[1])
    l_g = pltpu.make_async_copy(grads, big.at[me], loc.at[2])
    l_c = pltpu.make_async_copy(curv, curv_v, loc.at[3])
    l_r = pltpu.make_async_copy(right, right_v, loc.at[4])
    l_b = pltpu.make_async_copy(in_basis, ub_v, loc.at[5])
    l_a = pltpu.make_async_copy(acts.at[:, own_cols], cols.at[me], col_rs.at[me])
    for cp in (l_u, l_l, l_g, l_a, l_c, l_r, l_b):
        cp.start()

    barrier = pltpu.get_barrier_semaphore()

    def greet(o, _):
        pl.semaphore_signal(
            barrier, inc=1, device_id={"dp": (me + o) % n_dev}, device_id_type=MESH
        )
        return 0

    def greet_sec(o, _):
        pl.semaphore_signal(
            barrier, inc=1, device_id={"section": (sec + o) % n_sec}, device_id_type=MESH
        )
        return 0

    lax.fori_loop(1, n_dev, greet, 0)
    lax.fori_loop(1, n_sec, greet_sec, 0)
    rows_v[...] = jnp.zeros_like(rows_v)
    l_u.wait()
    l_l.wait()
    l_g.wait()
    pl.semaphore_wait(barrier, n_dev - 1 + n_sec - 1)

    counts = {"small": 0, "big": 0}
    parts = {"small": (small, small_ss, small_rs), "big": (big, big_ss, big_rs)}

    def copy_of(kind, which, s, dev):
        buf, ss, rs = parts[kind]
        return pltpu.make_async_remote_copy(
            src_ref=buf.at[s],
            dst_ref=buf.at[s],
            send_sem=ss.at[which],
            recv_sem=rs.at[s],
            device_id={"dp": dev},
            device_id_type=MESH,
        )

    def send(kind, s, dev):
        copy_of(kind, counts[kind], s, dev).start()
        counts[kind] += 1

    def landed(kind, s):
        copy_of(kind, 0, s, partner).wait_recv()

    steps = (0, -step, step, 2)

    def z_own(kind):
        send(kind, me, slot(1, 0, c))
        send(kind, me, slot(-1, 0, c))

    def spread(kind, g):
        s = slot(steps[g], 0, c)
        if g > 0:
            landed(kind, s)
        if g == 1:
            send(kind, s, slot(step, 0, c))
        send(kind, s, slot(0, 1, c))
        send(kind, s, slot(0, -1, c))
        send(kind, s, partner)

    def relay(kind, g):
        s = slot(steps[g], -step, c)
        landed(kind, s)
        send(kind, s, slot(0, step, c))
        send(kind, s, partner)
        s = slot(steps[g], step, c)
        landed(kind, s)
        send(kind, s, partner)

    def far(kind, g):
        s = slot(steps[g], 2, c)
        landed(kind, s)
        send(kind, s, partner)

    def other(kind, g):
        for dy in range(4):
            landed(kind, slot(steps[g], dy, 1 - c))

    def col_copy(dst, src_slot):
        return pltpu.make_async_remote_copy(
            src_ref=acts.at[:, pl.ds(pl.multiple_of(dst * width, width), width)],
            dst_ref=cols.at[src_slot],
            send_sem=col_ss.at[dst],
            recv_sem=col_rs.at[src_slot],
            device_id={"dp": dst},
            device_id_type=MESH,
        )

    def col_sends(dzs, lo, hi):
        def one(j, _):
            for dz in dzs:
                dst = ((z + dz + 8) % 4) * 8 + (sub + j) % 8
                col_copy(dst, me).start()
            return 0

        lax.fori_loop(lo, hi, one, 0)

    z_own("small")
    spread("small", 0)
    col_sends((1, -1), 0, 2)
    relay("small", 0)
    spread("small", 1)
    spread("small", 2)
    z_own("big")
    col_sends((1, -1), 2, 8)
    far("small", 0)
    relay("small", 1)
    relay("small", 2)
    spread("big", 0)
    col_sends((0,), 1, 8)
    l_c.wait()
    inv_v[...] = 1.0 / curv_v[...].astype(F32)
    l_r.wait()
    l_b.wait()
    far("small", 1)
    far("small", 2)
    relay("big", 0)
    spread("small", 3)
    relay("small", 3)
    far("big", 0)
    far("small", 3)
    for g in range(4):
        other("small", g)

    def lay(k, _):
        at = pl.ds(pl.multiple_of(k * 32, 32), 32)
        basis_v[at, :] = small[k, 0:32, :]
        left_v[at, :] = small[k, 32:64, :]
        return 0

    lax.fori_loop(0, n_dev, lay, 0)
    other("big", 0)

    ones = jnp.ones((8, 128), F32)

    def sequence(t, _):
        @pl.when(t == 4)
        def _():
            spread("big", 1)
            spread("big", 2)
            col_sends((2,), 0, 8)

        @pl.when(t == 8)
        def _():
            relay("big", 1)
            relay("big", 2)
            far("big", 1)
            far("big", 2)
            other("big", 1)
            other("big", 2)

        @pl.when(t == 20)
        def _():
            spread("big", 3)

        @pl.when(t == 22)
        def _():
            relay("big", 3)

        @pl.when(t == 24)
        def _():
            far("big", 3)
            other("big", 3)

        g = t // 8
        turn = ((g + 3) // 4) * (1 + (g + 1) % 3)
        zz = (z + step * turn + 16) % 4
        n = zz * 8 + (sub - t % 8 + 8) % 8
        col_copy(partner, n).wait_recv()
        acts_n = jnp.dot(cols[n], ub_v[...], preferred_element_type=F32).astype(BF16)
        for i in range(4):
            at = slice(i * 256, (i + 1) * 256)
            grads_n = jnp.dot(big[n], basis_v[:, at], preferred_element_type=F32).astype(BF16)
            gradient = lax.dot_general(
                grads_n, acts_n, (((0,), (0,)), ((), ())), preferred_element_type=F32
            )
            scaled_v[at, :] = (gradient * inv_v[at, :]).astype(BF16)
        for i in range(4):
            at = slice(i * 256, (i + 1) * 256)
            prod = jnp.dot(left_v[at, :], scaled_v[...], preferred_element_type=F32)
            prod = prod.reshape(8, 32, width) * right_v[i * 8 : (i + 1) * 8].astype(F32)
            summed = jnp.sum(prod, axis=1)
            part_v[i * 8 : (i + 1) * 8, :] = summed[:, :128] + summed[:, 128:]
        row = lax.dot_general(
            ones, part_v[...], (((1,), (1,)), ((), ())), precision=HI, preferred_element_type=F32
        )
        rows_v[pl.ds(n, 1), 0:32] = row[0:1]
        return 0

    lax.fori_loop(0, n_dev, sequence, 0)

    row_pick = (seq_ids[...] == lax.broadcasted_iota(jnp.int32, (32, 32), 0)).astype(F32)
    col_pick = (q_order[...] == lax.broadcasted_iota(jnp.int32, (32, 32), 0)).astype(F32)
    placed = jnp.dot(row_pick, rows_v[:, 0:32], precision=HI, preferred_element_type=F32)
    placed = lax.dot_general(
        placed, col_pick, (((1,), (1,)), ((), ())), precision=HI, preferred_element_type=F32
    )
    placed = jnp.concatenate([placed, jnp.zeros((32, 96), F32)], axis=1)
    for m in range(n_dev):
        row_send[m] = placed[m : m + 1]

    if counts != {"small": 31, "big": 31}:
        raise ValueError(str(counts))

    for kind in ("small", "big"):
        for i in range(counts[kind]):
            copy_of(kind, i, me, partner).wait_send()

    def col_left(o, _):
        col_copy((me + o) % n_dev, me).wait_send()
        return 0

    lax.fori_loop(1, n_dev, col_left, 0)

    def row_copy(dst, src_slot):
        return pltpu.make_async_remote_copy(
            src_ref=row_send.at[dst],
            dst_ref=row_recv.at[src_slot],
            send_sem=row_ss.at[dst],
            recv_sem=row_rs.at[src_slot],
            device_id={"dp": dst},
            device_id_type=MESH,
        )

    def row_start(o, _):
        row_copy((me + 15 + o) % n_dev, me).start()
        return 0

    lax.fori_loop(0, 17, row_start, 0)
    lax.fori_loop(18, n_dev, row_start, 0)
    row_recv[me] = row_send[me]

    def row_wait(o, _):
        row_copy(partner, (me + o) % n_dev).wait_recv()
        return 0

    lax.fori_loop(1, n_dev, row_wait, 0)
    total = jnp.sum(row_recv[...], axis=0)
    sec_send[...] = total

    def sec_copy(dst, src_slot):
        return pltpu.make_async_remote_copy(
            src_ref=sec_send,
            dst_ref=sec_recv.at[src_slot],
            send_sem=sec_ss.at[dst],
            recv_sem=sec_rs.at[src_slot],
            device_id={"section": dst},
            device_id_type=MESH,
        )

    def sec_start(o, _):
        sec_copy((sec + o) % n_sec, sec).start()
        return 0

    lax.fori_loop(1, n_sec, sec_start, 0)
    sec_recv[sec] = total

    def row_left(o, _):
        row_copy((me + o) % n_dev, me).wait_send()
        return 0

    lax.fori_loop(1, n_dev, row_left, 0)

    def sec_wait(o, _):
        sec_copy((sec + 1) % n_sec, (sec + o) % n_sec).wait_recv()
        sec_copy((sec + o) % n_sec, sec).wait_send()
        return 0

    lax.fori_loop(1, n_sec, sec_wait, 0)
    layer = lax.broadcasted_iota(jnp.int32, (n_sec, 1, 128), 0)
    kept = jnp.where(layer >= sec, sec_recv[...], 0.0)
    out[...] = jnp.sum(kept, axis=0)[:, 0:32]


def on_device(
    activations,
    out_grads,
    in_basis,
    out_basis,
    curvature,
    left_factors,
    right_factors,
    sequence_ids,
    query_order,
):
    hbm = pl.BlockSpec(memory_space=pl.ANY)
    vmem = pl.BlockSpec(memory_space=pltpu.VMEM)
    sems = pltpu.SemaphoreType.DMA
    total = pl.pallas_call(
        kernel,
        out_shape=jax.ShapeDtypeStruct((1, 32), F32),
        in_specs=[hbm] * 7 + [vmem] * 2,
        out_specs=vmem,
        scratch_shapes=[
            pltpu.VMEM((32, 64, 1024), BF16),
            pltpu.VMEM((32, 128, 1024), BF16),
            pltpu.VMEM((32, 128, 256), BF16),
            pltpu.VMEM((1024, 1024), BF16),
            pltpu.VMEM((1024, 1024), BF16),
            pltpu.VMEM((256, 256), BF16),
            pltpu.VMEM((1024, 256), BF16),
            pltpu.VMEM((1024, 256), F32),
            pltpu.VMEM((32, 32, 256), BF16),
            pltpu.VMEM((1024, 256), BF16),
            pltpu.VMEM((32, 128), F32),
            pltpu.VMEM((32, 128), F32),
            pltpu.VMEM((32, 1, 128), F32),
            pltpu.VMEM((32, 1, 128), F32),
            pltpu.VMEM((1, 128), F32),
            pltpu.VMEM((16, 1, 128), F32),
            sems((31,)),
            sems((32,)),
            sems((31,)),
            sems((32,)),
            sems((32,)),
            sems((32,)),
            sems((32,)),
            sems((32,)),
            sems((16,)),
            sems((16,)),
            sems((6,)),
        ],
        compiler_params=pltpu.CompilerParams(
            collective_id=0, has_side_effects=True, vmem_limit_bytes=56 * 2**20
        ),
        name="influence",
    )(
        activations[0],
        out_grads[0],
        in_basis[0],
        out_basis[0],
        curvature[0],
        left_factors[0, 0],
        right_factors[0],
        sequence_ids[None, :],
        query_order[None, :],
    )
    return total[None]


def solution(mesh):
    placed = (
        P("section", "dp", None),
        P("section", "dp", None),
        P("section", "dp", None),
        P("section", "dp", None),
        P("section", None, "dp"),
        P("section", "dp", None, None),
        P("section", None, None, "dp"),
        P(),
        P(),
    )
    return jax.shard_map(
        on_device, mesh=mesh, in_specs=placed, out_specs=P("section", "dp", None), check_vma=False
    )
```

```python
import jax
import jax.numpy as jnp
from jax import lax
from jax.experimental import pallas as pl
from jax.experimental.pallas import tpu as pltpu
from jax.sharding import PartitionSpec as P

MESH = pl.DeviceIdType.MESH
F32 = jnp.float32
BF16 = jnp.bfloat16
HI = lax.Precision.HIGHEST


def kernel(
    acts,
    grads,
    in_basis,
    out_basis,
    curv,
    left,
    right,
    seq_ids,
    q_order,
    out,
    small,
    big,
    cols,
    basis_v,
    rotated,
    left_v,
    ub_v,
    curv_v,
    inv_v,
    right_v,
    scaled_v,
    part_v,
    rows_v,
    row_send,
    row_recv,
    sec_send,
    sec_recv,
    small_ss,
    small_rs,
    big_ss,
    big_rs,
    col_ss,
    col_rs,
    row_ss,
    row_rs,
    sec_ss,
    sec_rs,
    loc,
):
    n_dev = 32
    n_sec = 16
    me = lax.axis_index("dp")
    sec = lax.axis_index("section")
    z = me // 8
    sub = me % 8
    y = sub // 2
    c = sub % 2
    step = 1 - 2 * c
    width = cols.shape[2]

    def slot(dz, dy, core):
        return ((z + dz + 8) % 4) * 8 + ((y + dy + 8) % 4) * 2 + core

    partner = slot(0, 0, 1 - c)

    own_cols = pl.ds(pl.multiple_of(me * width, width), width)
    l_u = pltpu.make_async_copy(out_basis, small.at[me, pl.ds(0, 32)], loc.at[0])
    l_l = pltpu.make_async_copy(left, small.at[me, pl.ds(32, 32)], loc.at[1])
    l_g = pltpu.make_async_copy(grads, big.at[me], loc.at[2])
    l_c = pltpu.make_async_copy(curv, curv_v, loc.at[3])
    l_r = pltpu.make_async_copy(right, right_v, loc.at[4])
    l_b = pltpu.make_async_copy(in_basis, ub_v, loc.at[5])
    l_a = pltpu.make_async_copy(acts.at[:, own_cols], cols.at[me], col_rs.at[me])
    for cp in (l_u, l_l, l_g, l_a, l_c, l_r, l_b):
        cp.start()

    barrier = pltpu.get_barrier_semaphore()

    def greet(o, _):
        pl.semaphore_signal(
            barrier, inc=1, device_id={"dp": (me + o) % n_dev}, device_id_type=MESH
        )
        return 0

    def greet_sec(o, _):
        pl.semaphore_signal(
            barrier, inc=1, device_id={"section": (sec + o) % n_sec}, device_id_type=MESH
        )
        return 0

    lax.fori_loop(1, n_dev, greet, 0)
    lax.fori_loop(1, n_sec, greet_sec, 0)
    rows_v[...] = jnp.zeros_like(rows_v)
    l_u.wait()
    l_l.wait()
    l_g.wait()
    pl.semaphore_wait(barrier, n_dev - 1 + n_sec - 1)

    counts = {"small": 0, "big": 0}
    parts = {"small": (small, small_ss, small_rs), "big": (big, big_ss, big_rs)}

    def copy_of(kind, which, s, dev):
        buf, ss, rs = parts[kind]
        return pltpu.make_async_remote_copy(
            src_ref=buf.at[s],
            dst_ref=buf.at[s],
            send_sem=ss.at[which],
            recv_sem=rs.at[s],
            device_id={"dp": dev},
            device_id_type=MESH,
        )

    def send(kind, s, dev):
        copy_of(kind, counts[kind], s, dev).start()
        counts[kind] += 1

    def landed(kind, s):
        copy_of(kind, 0, s, partner).wait_recv()

    steps = (0, -step, step, 2)

    def z_own(kind):
        send(kind, me, slot(1, 0, c))
        send(kind, me, slot(-1, 0, c))

    def spread(kind, g):
        s = slot(steps[g], 0, c)
        if g > 0:
            landed(kind, s)
        if g == 1:
            send(kind, s, slot(step, 0, c))
        send(kind, s, slot(0, 1, c))
        send(kind, s, slot(0, -1, c))
        send(kind, s, partner)

    def relay(kind, g):
        s = slot(steps[g], -step, c)
        landed(kind, s)
        send(kind, s, slot(0, step, c))
        send(kind, s, partner)
        s = slot(steps[g], step, c)
        landed(kind, s)
        send(kind, s, partner)

    def far(kind, g):
        s = slot(steps[g], 2, c)
        landed(kind, s)
        send(kind, s, partner)

    def other(kind, g):
        for dy in range(4):
            landed(kind, slot(steps[g], dy, 1 - c))

    def col_copy(dst, src_slot):
        return pltpu.make_async_remote_copy(
            src_ref=acts.at[:, pl.ds(pl.multiple_of(dst * width, width), width)],
            dst_ref=cols.at[src_slot],
            send_sem=col_ss.at[dst],
            recv_sem=col_rs.at[src_slot],
            device_id={"dp": dst},
            device_id_type=MESH,
        )

    def col_sends(dzs, lo, hi):
        def one(j, _):
            for dz in dzs:
                dst = slot(dz, j // 2, (c + j) % 2)
                col_copy(dst, me).start()
            return 0

        lax.fori_loop(lo, hi, one, 0)

    z_own("small")
    spread("small", 0)
    col_sends((1, -1), 0, 2)
    relay("small", 0)
    spread("big", 0)
    spread("small", 1)
    spread("small", 2)
    z_own("big")
    col_sends((1, -1), 2, 4)
    far("small", 0)
    relay("small", 1)
    relay("small", 2)
    col_sends((0,), 1, 8)
    l_c.wait()
    inv_v[...] = 1.0 / curv_v[...].astype(F32)
    l_r.wait()
    l_b.wait()
    far("small", 1)
    far("small", 2)
    spread("small", 3)
    relay("small", 3)
    relay("big", 0)
    far("big", 0)
    far("small", 3)
    for g in range(4):
        other("small", g)

    def lay(k, _):
        at = pl.ds(pl.multiple_of(k * 32, 32), 32)
        basis_v[at, :] = small[k, 0:32, :]
        left_v[at, :] = small[k, 32:64, :]
        return 0

    lax.fori_loop(0, n_dev, lay, 0)
    other("big", 0)

    ones = jnp.ones((8, 128), F32)

    def turn_of(g):
        return ((g + 3) // 4) * (1 + (g + 1) % 3)

    def rotate(g, _):
        at = pl.ds(pl.multiple_of(slot(step * turn_of(g), 0, 0) // 8 * 8, 8), 8)

        def chunk(i, _):
            to = pl.ds(pl.multiple_of(i * 256, 256), 256)
            turned = jnp.dot(
                big[at].reshape(1024, 1024), basis_v[:, to], preferred_element_type=F32
            )
            rotated[at, :, to] = turned.astype(BF16).reshape(8, 128, 256)
            return 0

        lax.fori_loop(0, 4, chunk, 0)
        return 0

    def sequence(t, _):
        @pl.when(t == 3)
        def _():
            spread("big", 1)
            spread("big", 2)
            col_sends((1, -1), 4, 8)
            col_sends((2,), 0, 8)

        @pl.when(t == 6)
        def _():
            relay("big", 1)
            relay("big", 2)

        @pl.when(t == 8)
        def _():
            far("big", 1)
            far("big", 2)
            other("big", 1)
            other("big", 2)

        @pl.when(t == 10)
        def _():
            spread("big", 3)

        @pl.when(t == 12)
        def _():
            relay("big", 3)

        @pl.when(t == 14)
        def _():
            far("big", 3)

        @pl.when(t == 16)
        def _():
            other("big", 3)

        @pl.when((t % 8 == 0) & (t < 24))
        def _():
            q = t // 8
            lax.fori_loop(q + q // 2, q + 1 + (q + 1) // 2, rotate, 0)

        turn = turn_of(t // 8)
        n = slot(step * turn, 4 - t % 8 // 2, (c + t) % 2)
        col_copy(partner, n).wait_recv()
        acts_n = jnp.dot(cols[n], ub_v[...], preferred_element_type=F32).astype(BF16)
        for i in range(4):
            at = slice(i * 256, (i + 1) * 256)
            gradient = lax.dot_general(
                rotated[n, :, at], acts_n, (((0,), (0,)), ((), ())), preferred_element_type=F32
            )
            scaled_v[at, :] = (gradient * inv_v[at, :]).astype(BF16)
        for i in range(4):
            at = slice(i * 256, (i + 1) * 256)
            prod = jnp.dot(left_v[at, :], scaled_v[...], preferred_element_type=F32)
            prod = prod.reshape(8, 32, width) * right_v[i * 8 : (i + 1) * 8].astype(F32)
            summed = jnp.sum(prod, axis=1)
            part_v[i * 8 : (i + 1) * 8, :] = summed[:, :128] + summed[:, 128:]
        row = lax.dot_general(
            ones, part_v[...], (((1,), (1,)), ((), ())), precision=HI, preferred_element_type=F32
        )
        rows_v[pl.ds(n, 1), 0:32] = row[0:1]
        return 0

    lax.fori_loop(0, n_dev, sequence, 0)

    row_pick = (seq_ids[...] == lax.broadcasted_iota(jnp.int32, (32, 32), 0)).astype(F32)
    col_pick = (q_order[...] == lax.broadcasted_iota(jnp.int32, (32, 32), 0)).astype(F32)
    placed = jnp.dot(row_pick, rows_v[:, 0:32], precision=HI, preferred_element_type=F32)
    placed = lax.dot_general(
        placed, col_pick, (((1,), (1,)), ((), ())), precision=HI, preferred_element_type=F32
    )
    placed = jnp.concatenate([placed, jnp.zeros((32, 96), F32)], axis=1)
    for m in range(n_dev):
        row_send[m] = placed[m : m + 1]

    if counts != {"small": 31, "big": 31}:
        raise ValueError(str(counts))

    for kind in ("small", "big"):
        for i in range(counts[kind]):
            copy_of(kind, i, me, partner).wait_send()

    def col_left(o, _):
        col_copy((me + o) % n_dev, me).wait_send()
        return 0

    lax.fori_loop(1, n_dev, col_left, 0)

    def row_copy(dst, src_slot):
        return pltpu.make_async_remote_copy(
            src_ref=row_send.at[dst],
            dst_ref=row_recv.at[src_slot],
            send_sem=row_ss.at[dst],
            recv_sem=row_rs.at[src_slot],
            device_id={"dp": dst},
            device_id_type=MESH,
        )

    def row_start(o, _):
        row_copy((me + 15 + o) % n_dev, me).start()
        return 0

    lax.fori_loop(0, 17, row_start, 0)
    lax.fori_loop(18, n_dev, row_start, 0)
    row_recv[me] = row_send[me]

    def row_wait(o, _):
        row_copy(partner, (me + o) % n_dev).wait_recv()
        return 0

    lax.fori_loop(1, n_dev, row_wait, 0)
    total = jnp.sum(row_recv[...], axis=0)
    sec_send[...] = total

    def sec_copy(dst, src_slot):
        return pltpu.make_async_remote_copy(
            src_ref=sec_send,
            dst_ref=sec_recv.at[src_slot],
            send_sem=sec_ss.at[dst],
            recv_sem=sec_rs.at[src_slot],
            device_id={"section": dst},
            device_id_type=MESH,
        )

    def sec_start(o, _):
        sec_copy((sec + o) % n_sec, sec).start()
        return 0

    lax.fori_loop(1, n_sec, sec_start, 0)
    sec_recv[sec] = total

    def row_left(o, _):
        row_copy((me + o) % n_dev, me).wait_send()
        return 0

    lax.fori_loop(1, n_dev, row_left, 0)

    def sec_wait(o, _):
        sec_copy((sec + 1) % n_sec, (sec + o) % n_sec).wait_recv()
        sec_copy((sec + o) % n_sec, sec).wait_send()
        return 0

    lax.fori_loop(1, n_sec, sec_wait, 0)
    layer = lax.broadcasted_iota(jnp.int32, (n_sec, 1, 128), 0)
    kept = jnp.where(layer >= sec, sec_recv[...], 0.0)
    out[...] = jnp.sum(kept, axis=0)[:, 0:32]


def on_device(
    activations,
    out_grads,
    in_basis,
    out_basis,
    curvature,
    left_factors,
    right_factors,
    sequence_ids,
    query_order,
):
    hbm = pl.BlockSpec(memory_space=pl.ANY)
    vmem = pl.BlockSpec(memory_space=pltpu.VMEM)
    sems = pltpu.SemaphoreType.DMA
    total = pl.pallas_call(
        kernel,
        out_shape=jax.ShapeDtypeStruct((1, 32), F32),
        in_specs=[hbm] * 7 + [vmem] * 2,
        out_specs=vmem,
        scratch_shapes=[
            pltpu.VMEM((32, 64, 1024), BF16),
            pltpu.VMEM((32, 128, 1024), BF16),
            pltpu.VMEM((32, 128, 256), BF16),
            pltpu.VMEM((1024, 1024), BF16),
            pltpu.VMEM((32, 128, 1024), BF16),
            pltpu.VMEM((1024, 1024), BF16),
            pltpu.VMEM((256, 256), BF16),
            pltpu.VMEM((1024, 256), BF16),
            pltpu.VMEM((1024, 256), F32),
            pltpu.VMEM((32, 32, 256), BF16),
            pltpu.VMEM((1024, 256), BF16),
            pltpu.VMEM((32, 128), F32),
            pltpu.VMEM((32, 128), F32),
            pltpu.VMEM((32, 1, 128), F32),
            pltpu.VMEM((32, 1, 128), F32),
            pltpu.VMEM((1, 128), F32),
            pltpu.VMEM((16, 1, 128), F32),
            sems((31,)),
            sems((32,)),
            sems((31,)),
            sems((32,)),
            sems((32,)),
            sems((32,)),
            sems((32,)),
            sems((32,)),
            sems((16,)),
            sems((16,)),
            sems((6,)),
        ],
        compiler_params=pltpu.CompilerParams(
            collective_id=0, has_side_effects=True, vmem_limit_bytes=56 * 2**20
        ),
        name="influence",
    )(
        activations[0],
        out_grads[0],
        in_basis[0],
        out_basis[0],
        curvature[0],
        left_factors[0, 0],
        right_factors[0],
        sequence_ids[None, :],
        query_order[None, :],
    )
    return total[None]


def solution(mesh):
    placed = (
        P("section", "dp", None),
        P("section", "dp", None),
        P("section", "dp", None),
        P("section", "dp", None),
        P("section", None, "dp"),
        P("section", "dp", None, None),
        P("section", None, None, "dp"),
        P(),
        P(),
    )
    return jax.shard_map(
        on_device, mesh=mesh, in_specs=placed, out_specs=P("section", "dp", None), check_vma=False
    )
```

```python
import jax
import jax.numpy as jnp
from jax import lax
from jax.experimental import pallas as pl
from jax.experimental.pallas import tpu as pltpu
from jax.sharding import PartitionSpec as P

MESH = pl.DeviceIdType.MESH
F32 = jnp.float32
BF16 = jnp.bfloat16
HI = lax.Precision.HIGHEST


def kernel(
    acts,
    grads,
    in_basis,
    out_basis,
    curv,
    left,
    right,
    seq_ids,
    q_order,
    out,
    small,
    big,
    cols,
    basis_v,
    rotated,
    left_v,
    ub_v,
    curv_v,
    inv_v,
    right_v,
    scaled_v,
    part_v,
    rows_v,
    row_send,
    row_recv,
    sec_send,
    sec_recv,
    small_ss,
    small_rs,
    big_ss,
    big_rs,
    col_ss,
    col_rs,
    row_ss,
    row_rs,
    sec_ss,
    sec_rs,
    loc,
    known,
):
    n_dev = 32
    n_sec = 16
    me = lax.axis_index("dp")
    sec = lax.axis_index("section")
    z = me // 8
    sub = me % 8
    y = sub // 2
    c = sub % 2
    step = 1 - 2 * c
    width = cols.shape[2]

    def slot(dz, dy, core):
        return ((z + dz + 8) % 4) * 8 + ((y + dy + 8) % 4) * 2 + core

    partner = slot(0, 0, 1 - c)

    own_cols = pl.ds(pl.multiple_of(me * width, width), width)
    l_u = pltpu.make_async_copy(out_basis, small.at[me, pl.ds(0, 32)], loc.at[0])
    l_l = pltpu.make_async_copy(left, small.at[me, pl.ds(32, 32)], loc.at[1])
    l_g = pltpu.make_async_copy(grads, big.at[me], loc.at[2])
    l_c = pltpu.make_async_copy(curv, curv_v, loc.at[3])
    l_r = pltpu.make_async_copy(right, right_v, loc.at[4])
    l_b = pltpu.make_async_copy(in_basis, ub_v, loc.at[5])
    l_a = pltpu.make_async_copy(acts.at[:, own_cols], cols.at[me], col_rs.at[me])
    for cp in (l_u, l_l, l_g, l_a, l_c, l_r, l_b):
        cp.start()

    barrier = pltpu.get_barrier_semaphore()

    def greet(dz):
        def one(j, _):
            pl.semaphore_signal(
                barrier,
                inc=1,
                device_id={"dp": slot(dz, j // 2, (c + j) % 2)},
                device_id_type=MESH,
            )
            return 0

        return one

    def greet_sec(o, _):
        pl.semaphore_signal(
            barrier, inc=1, device_id={"section": (sec + o) % n_sec}, device_id_type=MESH
        )
        return 0

    lax.fori_loop(0, 8, greet(1), 0)
    lax.fori_loop(0, 8, greet(-1), 0)
    lax.fori_loop(1, 8, greet(0), 0)
    lax.fori_loop(1, n_sec, greet_sec, 0)
    rows_v[...] = jnp.zeros_like(rows_v)
    l_u.wait()
    l_l.wait()
    l_g.wait()
    pl.semaphore_wait(barrier, 23 + n_sec - 1)
    pl.semaphore_signal(known, inc=1, device_id={"dp": slot(-1, 0, c)}, device_id_type=MESH)

    counts = {"small": 0, "big": 0}
    parts = {"small": (small, small_ss, small_rs), "big": (big, big_ss, big_rs)}

    def copy_of(kind, which, s, dev):
        buf, ss, rs = parts[kind]
        return pltpu.make_async_remote_copy(
            src_ref=buf.at[s],
            dst_ref=buf.at[s],
            send_sem=ss.at[which],
            recv_sem=rs.at[s],
            device_id={"dp": dev},
            device_id_type=MESH,
        )

    def send(kind, s, dev):
        copy_of(kind, counts[kind], s, dev).start()
        counts[kind] += 1

    def landed(kind, s):
        copy_of(kind, 0, s, partner).wait_recv()

    steps = (0, -step, step, 2)

    def z_own(kind):
        send(kind, me, slot(1, 0, c))
        send(kind, me, slot(-1, 0, c))

    def spread(kind, g):
        s = slot(steps[g], 0, c)
        if g > 0:
            landed(kind, s)
        if g == 1:
            send(kind, s, slot(step, 0, c))
        send(kind, s, slot(0, 1, c))
        send(kind, s, slot(0, -1, c))
        send(kind, s, partner)

    def relay(kind, g):
        s = slot(steps[g], -step, c)
        landed(kind, s)
        send(kind, s, slot(0, step, c))
        send(kind, s, partner)
        s = slot(steps[g], step, c)
        landed(kind, s)
        send(kind, s, partner)

    def far(kind, g):
        s = slot(steps[g], 2, c)
        landed(kind, s)
        send(kind, s, partner)

    def other(kind, g):
        for dy in range(4):
            landed(kind, slot(steps[g], dy, 1 - c))

    def col_copy(dst, src_slot):
        return pltpu.make_async_remote_copy(
            src_ref=acts.at[:, pl.ds(pl.multiple_of(dst * width, width), width)],
            dst_ref=cols.at[src_slot],
            send_sem=col_ss.at[dst],
            recv_sem=col_rs.at[src_slot],
            device_id={"dp": dst},
            device_id_type=MESH,
        )

    def col_sends(dzs, lo, hi):
        def one(j, _):
            for dz in dzs:
                dst = slot(dz, j // 2, (c + j) % 2)
                col_copy(dst, me).start()
            return 0

        lax.fori_loop(lo, hi, one, 0)

    z_own("small")
    spread("small", 0)
    col_sends((1, -1), 0, 2)
    relay("small", 0)
    spread("big", 0)
    spread("small", 1)
    spread("small", 2)
    z_own("big")
    col_sends((1, -1), 2, 4)
    far("small", 0)
    relay("small", 1)
    relay("small", 2)
    col_sends((0,), 1, 8)
    l_c.wait()
    inv_v[...] = 1.0 / curv_v[...].astype(F32)
    l_r.wait()
    l_b.wait()
    far("small", 1)
    far("small", 2)
    spread("small", 3)
    relay("small", 3)
    relay("big", 0)
    far("big", 0)
    far("small", 3)
    for g in range(4):
        other("small", g)

    def lay(k, _):
        at = pl.ds(pl.multiple_of(k * 32, 32), 32)
        basis_v[at, :] = small[k, 0:32, :]
        left_v[at, :] = small[k, 32:64, :]
        return 0

    lax.fori_loop(0, n_dev, lay, 0)
    pl.semaphore_wait(known, 1)
    other("big", 0)

    ones = jnp.ones((8, 128), F32)

    def turn_of(g):
        return ((g + 3) // 4) * (1 + (g + 1) % 3)

    def rotate(g, _):
        at = pl.ds(pl.multiple_of(slot(step * turn_of(g), 0, 0) // 8 * 8, 8), 8)

        def chunk(i, _):
            to = pl.ds(pl.multiple_of(i * 256, 256), 256)
            turned = jnp.dot(
                big[at].reshape(1024, 1024), basis_v[:, to], preferred_element_type=F32
            )
            rotated[at, :, to] = turned.astype(BF16).reshape(8, 128, 256)
            return 0

        lax.fori_loop(0, 4, chunk, 0)
        return 0

    def sequence(t, _):
        @pl.when(t == 3)
        def _():
            spread("big", 1)
            spread("big", 2)
            col_sends((2,), 0, 8)

        @pl.when(t == 3 + 9 * (sec % 4 // 2))
        def _():
            col_sends((1, -1), 4, 8)

        @pl.when(t == 6)
        def _():
            relay("big", 1)
            relay("big", 2)

        @pl.when(t == 8)
        def _():
            far("big", 1)
            far("big", 2)
            other("big", 1)
            other("big", 2)

        @pl.when(t == 10)
        def _():
            spread("big", 3)

        @pl.when(t == 12)
        def _():
            relay("big", 3)

        @pl.when(t == 14)
        def _():
            far("big", 3)

        @pl.when(t == 16)
        def _():
            other("big", 3)

        @pl.when((t % 8 == 0) & (t < 24))
        def _():
            q = t // 8
            lax.fori_loop(q + q // 2, q + 1 + (q + 1) // 2, rotate, 0)

        @pl.when(t == 26)
        def _():
            for kind in ("small", "big"):
                for i in range(counts[kind]):
                    copy_of(kind, i, me, partner).wait_send()

        u = t // 4
        half = (u + 3) // 8 + ((u + 7) // 8) * ((9 - u) // 8)
        r = (u + 2) % 4
        turn = ((u + 6) // 8) * ((1 - r // 2) * (3 - 2 * r) + 2 * (r // 2))
        j = half * 4 + t % 4
        n = slot(step * turn, 4 - j // 2, (c + j) % 2)
        col_copy(partner, n).wait_recv()
        acts_n = jnp.dot(cols[n], ub_v[...], preferred_element_type=F32).astype(BF16)
        for i in range(4):
            at = slice(i * 256, (i + 1) * 256)
            gradient = lax.dot_general(
                rotated[n, :, at], acts_n, (((0,), (0,)), ((), ())), preferred_element_type=F32
            )
            scaled_v[at, :] = (gradient * inv_v[at, :]).astype(BF16)
        for i in range(4):
            at = slice(i * 256, (i + 1) * 256)
            prod = jnp.dot(left_v[at, :], scaled_v[...], preferred_element_type=F32)
            prod = prod.reshape(8, 32, width) * right_v[i * 8 : (i + 1) * 8].astype(F32)
            summed = jnp.sum(prod, axis=1)
            part_v[i * 8 : (i + 1) * 8, :] = summed[:, :128] + summed[:, 128:]
        row = lax.dot_general(
            ones, part_v[...], (((1,), (1,)), ((), ())), precision=HI, preferred_element_type=F32
        )
        rows_v[pl.ds(n, 1), 0:32] = row[0:1]
        return 0

    lax.fori_loop(0, n_dev, sequence, 0)

    row_pick = (seq_ids[...] == lax.broadcasted_iota(jnp.int32, (32, 32), 0)).astype(F32)
    col_pick = (q_order[...] == lax.broadcasted_iota(jnp.int32, (32, 32), 0)).astype(F32)
    placed = jnp.dot(row_pick, rows_v[:, 0:32], precision=HI, preferred_element_type=F32)
    placed = lax.dot_general(
        placed, col_pick, (((1,), (1,)), ((), ())), precision=HI, preferred_element_type=F32
    )
    placed = jnp.concatenate([placed, jnp.zeros((32, 96), F32)], axis=1)
    for m in range(n_dev):
        row_send[m] = placed[m : m + 1]

    if counts != {"small": 31, "big": 31}:
        raise ValueError(str(counts))

    def col_left(o, _):
        col_copy((me + o) % n_dev, me).wait_send()
        return 0

    lax.fori_loop(1, n_dev, col_left, 0)

    def row_copy(dst, src_slot):
        return pltpu.make_async_remote_copy(
            src_ref=row_send.at[dst],
            dst_ref=row_recv.at[src_slot],
            send_sem=row_ss.at[dst],
            recv_sem=row_rs.at[src_slot],
            device_id={"dp": dst},
            device_id_type=MESH,
        )

    def row_start(o, _):
        row_copy((me + 15 + o) % n_dev, me).start()
        return 0

    lax.fori_loop(0, 17, row_start, 0)
    lax.fori_loop(18, n_dev, row_start, 0)
    row_recv[me] = row_send[me]

    def row_wait(o, _):
        row_copy(partner, (me + o) % n_dev).wait_recv()
        return 0

    lax.fori_loop(1, n_dev, row_wait, 0)
    total = jnp.sum(row_recv[...], axis=0)
    sec_send[...] = total

    def sec_copy(dst, src_slot):
        return pltpu.make_async_remote_copy(
            src_ref=sec_send,
            dst_ref=sec_recv.at[src_slot],
            send_sem=sec_ss.at[dst],
            recv_sem=sec_rs.at[src_slot],
            device_id={"section": dst},
            device_id_type=MESH,
        )

    def sec_start(o, _):
        sec_copy((sec + o) % n_sec, sec).start()
        return 0

    lax.fori_loop(1, n_sec, sec_start, 0)
    sec_recv[sec] = total

    def row_left(o, _):
        row_copy((me + o) % n_dev, me).wait_send()
        return 0

    lax.fori_loop(1, n_dev, row_left, 0)

    def sec_wait(o, _):
        sec_copy((sec + 1) % n_sec, (sec + o) % n_sec).wait_recv()
        sec_copy((sec + o) % n_sec, sec).wait_send()
        return 0

    lax.fori_loop(1, n_sec, sec_wait, 0)
    layer = lax.broadcasted_iota(jnp.int32, (n_sec, 1, 128), 0)
    kept = jnp.where(layer >= sec, sec_recv[...], 0.0)
    out[...] = jnp.sum(kept, axis=0)[:, 0:32]


def on_device(
    activations,
    out_grads,
    in_basis,
    out_basis,
    curvature,
    left_factors,
    right_factors,
    sequence_ids,
    query_order,
):
    hbm = pl.BlockSpec(memory_space=pl.ANY)
    vmem = pl.BlockSpec(memory_space=pltpu.VMEM)
    sems = pltpu.SemaphoreType.DMA
    total = pl.pallas_call(
        kernel,
        out_shape=jax.ShapeDtypeStruct((1, 32), F32),
        in_specs=[hbm] * 7 + [vmem] * 2,
        out_specs=vmem,
        scratch_shapes=[
            pltpu.VMEM((32, 64, 1024), BF16),
            pltpu.VMEM((32, 128, 1024), BF16),
            pltpu.VMEM((32, 128, 256), BF16),
            pltpu.VMEM((1024, 1024), BF16),
            pltpu.VMEM((32, 128, 1024), BF16),
            pltpu.VMEM((1024, 1024), BF16),
            pltpu.VMEM((256, 256), BF16),
            pltpu.VMEM((1024, 256), BF16),
            pltpu.VMEM((1024, 256), F32),
            pltpu.VMEM((32, 32, 256), BF16),
            pltpu.VMEM((1024, 256), BF16),
            pltpu.VMEM((32, 128), F32),
            pltpu.VMEM((32, 128), F32),
            pltpu.VMEM((32, 1, 128), F32),
            pltpu.VMEM((32, 1, 128), F32),
            pltpu.VMEM((1, 128), F32),
            pltpu.VMEM((16, 1, 128), F32),
            sems((31,)),
            sems((32,)),
            sems((31,)),
            sems((32,)),
            sems((32,)),
            sems((32,)),
            sems((32,)),
            sems((32,)),
            sems((16,)),
            sems((16,)),
            sems((6,)),
            pltpu.SemaphoreType.REGULAR,
        ],
        compiler_params=pltpu.CompilerParams(
            collective_id=0, has_side_effects=True, vmem_limit_bytes=56 * 2**20
        ),
        name="influence",
    )(
        activations[0],
        out_grads[0],
        in_basis[0],
        out_basis[0],
        curvature[0],
        left_factors[0, 0],
        right_factors[0],
        sequence_ids[None, :],
        query_order[None, :],
    )
    return total[None]


def solution(mesh):
    placed = (
        P("section", "dp", None),
        P("section", "dp", None),
        P("section", "dp", None),
        P("section", "dp", None),
        P("section", None, "dp"),
        P("section", "dp", None, None),
        P("section", None, None, "dp"),
        P(),
        P(),
    )
    return jax.shard_map(
        on_device, mesh=mesh, in_specs=placed, out_specs=P("section", "dp", None), check_vma=False
    )
```

```python
import jax
import jax.numpy as jnp
from jax import lax
from jax.experimental import pallas as pl
from jax.experimental.pallas import tpu as pltpu
from jax.sharding import PartitionSpec as P

MESH = pl.DeviceIdType.MESH
F32 = jnp.float32
BF16 = jnp.bfloat16
HI = lax.Precision.HIGHEST


def kernel(
    acts,
    grads,
    in_basis,
    out_basis,
    curv,
    left,
    right,
    seq_ids,
    q_order,
    out,
    small,
    big,
    cols,
    basis_v,
    rotated,
    left_v,
    ub_v,
    curv_v,
    inv_v,
    right_v,
    scaled_v,
    part_v,
    rows_v,
    row_send,
    row_recv,
    sec_send,
    sec_recv,
    small_ss,
    small_rs,
    big_ss,
    big_rs,
    col_ss,
    col_rs,
    row_ss,
    row_rs,
    sec_ss,
    sec_rs,
    loc,
):
    n_dev = 32
    n_sec = 16
    me = lax.axis_index("dp")
    sec = lax.axis_index("section")
    z = me // 8
    sub = me % 8
    y = sub // 2
    c = sub % 2
    step = 1 - 2 * c
    width = cols.shape[2]

    def slot(dz, dy, core):
        return ((z + dz + 8) % 4) * 8 + ((y + dy + 8) % 4) * 2 + core

    partner = slot(0, 0, 1 - c)

    own_cols = pl.ds(pl.multiple_of(me * width, width), width)
    l_u = pltpu.make_async_copy(out_basis, small.at[me, pl.ds(0, 32)], loc.at[0])
    l_l = pltpu.make_async_copy(left, small.at[me, pl.ds(32, 32)], loc.at[1])
    l_g = pltpu.make_async_copy(grads, big.at[me], loc.at[2])
    l_c = pltpu.make_async_copy(curv, curv_v, loc.at[3])
    l_r = pltpu.make_async_copy(right, right_v, loc.at[4])
    l_b = pltpu.make_async_copy(in_basis, ub_v, loc.at[5])
    l_a = pltpu.make_async_copy(acts.at[:, own_cols], cols.at[me], col_rs.at[me])
    for cp in (l_u, l_l, l_g, l_a, l_c, l_r, l_b):
        cp.start()

    barrier = pltpu.get_barrier_semaphore()

    def greet(o, _):
        pl.semaphore_signal(
            barrier, inc=1, device_id={"dp": (me + o) % n_dev}, device_id_type=MESH
        )
        return 0

    def greet_sec(o, _):
        pl.semaphore_signal(
            barrier, inc=1, device_id={"section": (sec + o) % n_sec}, device_id_type=MESH
        )
        return 0

    lax.fori_loop(1, n_dev, greet, 0)
    lax.fori_loop(1, n_sec, greet_sec, 0)
    rows_v[...] = jnp.zeros_like(rows_v)
    l_u.wait()
    l_l.wait()
    l_g.wait()
    pl.semaphore_wait(barrier, n_dev - 1 + n_sec - 1)

    counts = {"small": 0, "big": 0}
    parts = {"small": (small, small_ss, small_rs), "big": (big, big_ss, big_rs)}

    def copy_of(kind, which, s, dev):
        buf, ss, rs = parts[kind]
        return pltpu.make_async_remote_copy(
            src_ref=buf.at[s],
            dst_ref=buf.at[s],
            send_sem=ss.at[which],
            recv_sem=rs.at[s],
            device_id={"dp": dev},
            device_id_type=MESH,
        )

    def send(kind, s, dev):
        copy_of(kind, counts[kind], s, dev).start()
        counts[kind] += 1

    def landed(kind, s):
        copy_of(kind, 0, s, partner).wait_recv()

    steps = (0, -step, step, 2)

    def z_own(kind):
        send(kind, me, slot(1, 0, c))
        send(kind, me, slot(-1, 0, c))

    def spread(kind, g):
        s = slot(steps[g], 0, c)
        if g > 0:
            landed(kind, s)
        if g == 1:
            send(kind, s, slot(step, 0, c))
        send(kind, s, slot(0, 1, c))
        send(kind, s, slot(0, -1, c))
        send(kind, s, partner)

    def relay(kind, g):
        s = slot(steps[g], -step, c)
        landed(kind, s)
        send(kind, s, slot(0, step, c))
        send(kind, s, partner)
        s = slot(steps[g], step, c)
        landed(kind, s)
        send(kind, s, partner)

    def far(kind, g):
        s = slot(steps[g], 2, c)
        landed(kind, s)
        send(kind, s, partner)

    def other(kind, g):
        for dy in range(4):
            landed(kind, slot(steps[g], dy, 1 - c))

    def col_copy(dst, src_slot):
        return pltpu.make_async_remote_copy(
            src_ref=acts.at[:, pl.ds(pl.multiple_of(dst * width, width), width)],
            dst_ref=cols.at[src_slot],
            send_sem=col_ss.at[dst],
            recv_sem=col_rs.at[src_slot],
            device_id={"dp": dst},
            device_id_type=MESH,
        )

    def col_sends(dzs, lo, hi):
        def one(j, _):
            for dz in dzs:
                dst = slot(dz, j // 2, (c + j) % 2)
                col_copy(dst, me).start()
            return 0

        lax.fori_loop(lo, hi, one, 0)

    z_own("small")
    spread("small", 0)
    col_sends((1, -1), 0, 2)
    relay("small", 0)
    spread("big", 0)
    spread("small", 1)
    spread("small", 2)
    z_own("big")
    col_sends((1, -1), 2, 4)
    far("small", 0)
    relay("small", 1)
    relay("small", 2)
    col_sends((0,), 1, 8)
    l_c.wait()
    inv_v[...] = 1.0 / curv_v[...].astype(F32)
    l_r.wait()
    l_b.wait()
    far("small", 1)
    far("small", 2)
    spread("small", 3)
    relay("small", 3)
    relay("big", 0)
    far("big", 0)
    far("small", 3)
    for g in range(4):
        other("small", g)

    def lay(k, _):
        at = pl.ds(pl.multiple_of(k * 32, 32), 32)
        basis_v[at, :] = small[k, 0:32, :]
        left_v[at, :] = small[k, 32:64, :]
        return 0

    lax.fori_loop(0, n_dev, lay, 0)
    other("big", 0)

    ones = jnp.ones((8, 128), F32)

    def turn_of(g):
        return ((g + 3) // 4) * (1 + (g + 1) % 3)

    def rotate(g, _):
        at = pl.ds(pl.multiple_of(slot(step * turn_of(g), 0, 0) // 8 * 8, 8), 8)

        def chunk(i, _):
            to = pl.ds(pl.multiple_of(i * 256, 256), 256)
            turned = jnp.dot(
                big[at].reshape(1024, 1024), basis_v[:, to], preferred_element_type=F32
            )
            rotated[at, :, to] = turned.astype(BF16).reshape(8, 128, 256)
            return 0

        lax.fori_loop(0, 4, chunk, 0)
        return 0

    def sequence(t, _):
        @pl.when(t == 3)
        def _():
            spread("big", 1)
            spread("big", 2)
            col_sends((2,), 0, 8)

        @pl.when(t == 3 + 9 * (sec % 4 // 2))
        def _():
            col_sends((1, -1), 4, 8)

        @pl.when(t == 6)
        def _():
            relay("big", 1)
            relay("big", 2)

        @pl.when(t == 8)
        def _():
            far("big", 1)
            far("big", 2)
            other("big", 1)
            other("big", 2)

        @pl.when(t == 10)
        def _():
            spread("big", 3)

        @pl.when(t == 12)
        def _():
            relay("big", 3)

        @pl.when(t == 14)
        def _():
            far("big", 3)

        @pl.when(t == 16)
        def _():
            other("big", 3)

        @pl.when((t % 8 == 0) & (t < 24))
        def _():
            q = t // 8
            lax.fori_loop(q + q // 2, q + 1 + (q + 1) // 2, rotate, 0)

        @pl.when(t == 26)
        def _():
            for kind in ("small", "big"):
                for i in range(counts[kind]):
                    copy_of(kind, i, me, partner).wait_send()

        u = t // 4
        half = (u + 3) // 8 + ((u + 7) // 8) * ((9 - u) // 8)
        r = (u + 2) % 4
        turn = ((u + 6) // 8) * ((1 - r // 2) * (3 - 2 * r) + 2 * (r // 2))
        j = half * 4 + t % 4
        n = slot(step * turn, 4 - j // 2, (c + j) % 2)
        col_copy(partner, n).wait_recv()
        acts_n = jnp.dot(cols[n], ub_v[...], preferred_element_type=F32).astype(BF16)
        for i in range(4):
            at = slice(i * 256, (i + 1) * 256)
            gradient = lax.dot_general(
                rotated[n, :, at], acts_n, (((0,), (0,)), ((), ())), preferred_element_type=F32
            )
            scaled_v[at, :] = (gradient * inv_v[at, :]).astype(BF16)
        for i in range(4):
            at = slice(i * 256, (i + 1) * 256)
            prod = jnp.dot(left_v[at, :], scaled_v[...], preferred_element_type=F32)
            prod = prod.reshape(8, 32, width) * right_v[i * 8 : (i + 1) * 8].astype(F32)
            summed = jnp.sum(prod, axis=1)
            part_v[i * 8 : (i + 1) * 8, :] = summed[:, :128] + summed[:, 128:]
        row = lax.dot_general(
            ones, part_v[...], (((1,), (1,)), ((), ())), precision=HI, preferred_element_type=F32
        )
        rows_v[pl.ds(n, 1), 0:32] = row[0:1]
        return 0

    lax.fori_loop(0, n_dev, sequence, 0)

    row_pick = (seq_ids[...] == lax.broadcasted_iota(jnp.int32, (32, 32), 0)).astype(F32)
    col_pick = (q_order[...] == lax.broadcasted_iota(jnp.int32, (32, 32), 0)).astype(F32)
    placed = jnp.dot(row_pick, rows_v[:, 0:32], precision=HI, preferred_element_type=F32)
    placed = lax.dot_general(
        placed, col_pick, (((1,), (1,)), ((), ())), precision=HI, preferred_element_type=F32
    )
    placed = jnp.concatenate([placed, jnp.zeros((32, 96), F32)], axis=1)
    for m in range(n_dev):
        row_send[m] = placed[m : m + 1]

    if counts != {"small": 31, "big": 31}:
        raise ValueError(str(counts))

    def col_left(o, _):
        col_copy((me + o) % n_dev, me).wait_send()
        return 0

    lax.fori_loop(1, n_dev, col_left, 0)

    def row_copy(dst, src_slot):
        return pltpu.make_async_remote_copy(
            src_ref=row_send.at[dst],
            dst_ref=row_recv.at[src_slot],
            send_sem=row_ss.at[dst],
            recv_sem=row_rs.at[src_slot],
            device_id={"dp": dst},
            device_id_type=MESH,
        )

    def row_start(o, _):
        row_copy((me + 15 + o) % n_dev, me).start()
        return 0

    lax.fori_loop(0, 17, row_start, 0)
    lax.fori_loop(18, n_dev, row_start, 0)
    row_recv[me] = row_send[me]

    def row_wait(o, _):
        row_copy(partner, (me + o) % n_dev).wait_recv()
        return 0

    lax.fori_loop(1, n_dev, row_wait, 0)
    total = jnp.sum(row_recv[...], axis=0)
    sec_send[...] = total

    def sec_copy(dst, src_slot):
        return pltpu.make_async_remote_copy(
            src_ref=sec_send,
            dst_ref=sec_recv.at[src_slot],
            send_sem=sec_ss.at[dst],
            recv_sem=sec_rs.at[src_slot],
            device_id={"section": dst},
            device_id_type=MESH,
        )

    def sec_start(o, _):
        sec_copy((sec + o) % n_sec, sec).start()
        return 0

    lax.fori_loop(1, n_sec, sec_start, 0)
    sec_recv[sec] = total

    def row_left(o, _):
        row_copy((me + o) % n_dev, me).wait_send()
        return 0

    lax.fori_loop(1, n_dev, row_left, 0)

    def sec_wait(o, _):
        sec_copy((sec + 1) % n_sec, (sec + o) % n_sec).wait_recv()
        sec_copy((sec + o) % n_sec, sec).wait_send()
        return 0

    lax.fori_loop(1, n_sec, sec_wait, 0)
    layer = lax.broadcasted_iota(jnp.int32, (n_sec, 1, 128), 0)
    kept = jnp.where(layer >= sec, sec_recv[...], 0.0)
    out[...] = jnp.sum(kept, axis=0)[:, 0:32]


def on_device(
    activations,
    out_grads,
    in_basis,
    out_basis,
    curvature,
    left_factors,
    right_factors,
    sequence_ids,
    query_order,
):
    hbm = pl.BlockSpec(memory_space=pl.ANY)
    vmem = pl.BlockSpec(memory_space=pltpu.VMEM)
    sems = pltpu.SemaphoreType.DMA
    total = pl.pallas_call(
        kernel,
        out_shape=jax.ShapeDtypeStruct((1, 32), F32),
        in_specs=[hbm] * 7 + [vmem] * 2,
        out_specs=vmem,
        scratch_shapes=[
            pltpu.VMEM((32, 64, 1024), BF16),
            pltpu.VMEM((32, 128, 1024), BF16),
            pltpu.VMEM((32, 128, 256), BF16),
            pltpu.VMEM((1024, 1024), BF16),
            pltpu.VMEM((32, 128, 1024), BF16),
            pltpu.VMEM((1024, 1024), BF16),
            pltpu.VMEM((256, 256), BF16),
            pltpu.VMEM((1024, 256), BF16),
            pltpu.VMEM((1024, 256), F32),
            pltpu.VMEM((32, 32, 256), BF16),
            pltpu.VMEM((1024, 256), BF16),
            pltpu.VMEM((32, 128), F32),
            pltpu.VMEM((32, 128), F32),
            pltpu.VMEM((32, 1, 128), F32),
            pltpu.VMEM((32, 1, 128), F32),
            pltpu.VMEM((1, 128), F32),
            pltpu.VMEM((16, 1, 128), F32),
            sems((31,)),
            sems((32,)),
            sems((31,)),
            sems((32,)),
            sems((32,)),
            sems((32,)),
            sems((32,)),
            sems((32,)),
            sems((16,)),
            sems((16,)),
            sems((6,)),
        ],
        compiler_params=pltpu.CompilerParams(
            collective_id=0, has_side_effects=True, vmem_limit_bytes=56 * 2**20
        ),
        name="influence",
    )(
        activations[0],
        out_grads[0],
        in_basis[0],
        out_basis[0],
        curvature[0],
        left_factors[0, 0],
        right_factors[0],
        sequence_ids[None, :],
        query_order[None, :],
    )
    return total[None]


def solution(mesh):
    placed = (
        P("section", "dp", None),
        P("section", "dp", None),
        P("section", "dp", None),
        P("section", "dp", None),
        P("section", None, "dp"),
        P("section", "dp", None, None),
        P("section", None, None, "dp"),
        P(),
        P(),
    )
    return jax.shard_map(
        on_device, mesh=mesh, in_specs=placed, out_specs=P("section", "dp", None), check_vma=False
    )
```
